32 devices in a mesh: prow: 8 (over z, core), pcol: 4 (over y, x).
Axes of the slice: x: 2, y: 2, z: 4, core: 2. Of those that a mesh axis runs over, the one named last changes fastest.
Arguments:
- tri_corners: float32 [9, 2048], P(None, ('prow', 'pcol')), may hold values from -1.6 to 1.6, as said below
- edge_tris: int32 [2, 2048], P(None, 'prow'), may hold values from 0 to 2047, as said below
- edge_free: int32 [2, 2048], P(None, 'prow'), may hold values from 0 to 2
- pivots: int32 [1, 256], replicated, may hold values from 0 to 2047, as said below
- lower_inv: float32 [1, 2, 256, 256], P(None, None, 'prow'), may hold values from -1 to 1, as said below
- upper_inv: float32 [1, 2, 256, 256], P(None, None, 'prow'), may hold values from -2 to 2, as said below
Outputs:
- slab_matrix: float32 [2048, 1024], P('prow', 'pcol')
The draws below stay inside these ranges and needn't reach their ends.
Inputs may be any that keep to these rules, and one draw needn't show every extreme that they name: `tri_corners`: corners of triangles of area 0.0035 or more. `edge_tris`: the two triangles of edge m differ and both lie in [256 (m // 256), 256 (m // 256) + 256); in each such block every triangle is the plus triangle of exactly one edge. pivots[p, i] is 256 p + i or at least 256 (p + 1); the entries of pivots[p] are distinct. `lower_inv`: each panel's complex matrix is lower triangular with unit diagonal. `upper_inv`: each panel's complex matrix is upper triangular with diagonal entries of modulus 0.5 to 2.
All inputs are finite; a program needn't handle non-finite values.
Results may differ from the reference program's by a relative error of at most 0.0003.
Values sent between devices are 32-bit elements; how exact they have to be, the bound alone decides.
No kernel may reach another device: no remote copies, remote signals or barrier semaphores. Data moves between devices by JAX's collectives and lax.ppermute only.
A program may use at most 64 MiB of HBM per device.

```python
import math
import jax
import jax.numpy as jnp
from jax import lax

R_DEV = 256
SLAB = 512
PW = 256
PANELS = 1
ROWS = 2048
TRIANGLES = 2048
N_PROW = 8
N_PCOL = 4


def draw_tri_corners(key, part):
    subkeys = jax.random.split(key, 6)
    total_count = TRIANGLES
    lower_corner = jnp.full((3,), -1.0, jnp.float32)
    extent = jnp.full((3,), 2.0, jnp.float32)
    centre = lower_corner[:, None] + extent[:, None] * jax.random.uniform(subkeys[0], (3, total_count), jnp.float32)
    azimuth = jax.random.uniform(subkeys[1], (total_count,), jnp.float32, -math.pi, math.pi)
    elevation = jax.random.uniform(subkeys[2], (total_count,), jnp.float32, -0.5 * math.pi, 0.5 * math.pi)
    rotation = jax.random.uniform(subkeys[3], (total_count,), jnp.float32, -math.pi, math.pi)
    radius = jax.random.uniform(subkeys[4], (3, total_count), jnp.float32, 0.07, 0.1)
    jitter = jax.random.uniform(subkeys[5], (3, total_count), jnp.float32, -0.25, 0.25)
    first_axis = jnp.stack([-jnp.sin(azimuth), jnp.cos(azimuth), jnp.zeros_like(azimuth)])
    second_axis = jnp.stack([-jnp.cos(azimuth) * jnp.sin(elevation), -jnp.sin(azimuth) * jnp.sin(elevation), jnp.cos(elevation)])
    corners = []
    for corner_index in range(3):
        corner_angle = rotation + 2.0 * math.pi * corner_index / 3.0 + jitter[corner_index]
        corners.append(centre + radius[corner_index] * (jnp.cos(corner_angle) * first_axis + jnp.sin(corner_angle) * second_axis))
    return jnp.concatenate(corners, axis=0)


def draw_edge_tris(key, part):
    block_count = ROWS // R_DEV
    block_keys = jax.random.split(key, block_count)
    plus_local = jax.vmap(lambda member: jax.random.permutation(member, R_DEV))(block_keys).astype(jnp.int32)
    step_size = jax.random.randint(jax.random.fold_in(key, 7), (block_count, R_DEV), 1, R_DEV, dtype=jnp.int32)
    minus_local = (plus_local + step_size) % R_DEV
    base_index = (jnp.arange(block_count, dtype=jnp.int32) * R_DEV)[:, None]
    return jnp.stack([(plus_local + base_index).reshape(ROWS), (minus_local + base_index).reshape(ROWS)]).astype(jnp.int32)


def draw_pivots(key, part):
    rows_out = []
    for panel_number in range(PANELS):
        panel_start = panel_number * PW
        panel_key = jax.random.fold_in(key, panel_number)
        candidate = jax.random.permutation(jax.random.fold_in(panel_key, 1), ROWS - panel_start - PW)[:PW]
        candidate = candidate.astype(jnp.int32) + panel_start + PW
        swapping = jax.random.randint(jax.random.fold_in(panel_key, 2), (PW,), 0, 4, dtype=jnp.int32) > 0
        rows_out.append(jnp.where(swapping, candidate, panel_start + jnp.arange(PW, dtype=jnp.int32)))
    return jnp.stack(rows_out).astype(jnp.int32)


def draw_lower_inv(key, part):
    subkeys = jax.random.split(key, 1)
    shape_full = (PANELS, 2, PW, PW)
    spread = 0.7 * jax.random.truncated_normal(subkeys[0], -4.0, 4.0, shape_full, jnp.float32)
    position = jnp.arange(PW)
    strict = (position[:, None] > position[None, :]).astype(jnp.float32)
    identity = (position[:, None] == position[None, :]).astype(jnp.float32)
    part_one = jnp.array([1.0, 0.0], jnp.float32)[None, :, None, None]
    return spread * strict / math.sqrt(PW) + identity * part_one


def draw_upper_inv(key, part):
    subkeys = jax.random.split(key, 3)
    shape_full = (PANELS, 2, PW, PW)
    spread = jax.random.truncated_normal(subkeys[0], -4.0, 4.0, shape_full, jnp.float32)
    magnitude = jnp.exp(jax.random.uniform(subkeys[1], (PANELS, PW), jnp.float32, math.log(0.5), math.log(2.0)))
    rotation = jax.random.uniform(subkeys[2], (PANELS, PW), jnp.float32, -math.pi, math.pi)
    diagonal = jnp.stack([magnitude * jnp.cos(rotation), magnitude * jnp.sin(rotation)], axis=1)
    position = jnp.arange(PW)
    strict = (position[:, None] < position[None, :]).astype(jnp.float32)
    identity = (position[:, None] == position[None, :]).astype(jnp.float32)
    return spread * strict / math.sqrt(PW) + identity[None, None] * diagonal[:, :, :, None]


def set_ends(values, stream_key, low, top_value):
    spot = [jax.random.randint(jax.random.fold_in(stream_key, axis), (), 0, length) for axis, length in enumerate(values.shape)]
    longest = values.shape.index(max(values.shape))
    beside = spot[:longest] + [(spot[longest] + 1) % values.shape[longest]] + spot[longest + 1:]
    return values.at[tuple(spot)].set(low).at[tuple(beside)].set(top_value)


def setup_inputs(seed: int = 0) -> dict:
    key_of = jax.random.split(jax.random.key(seed), 7)
    return {
        "tri_corners": draw_tri_corners(jax.random.fold_in(key_of[6], 71), 0),
        "edge_tris": draw_edge_tris(jax.random.fold_in(key_of[6], 71), 0),
        "edge_free": set_ends(jax.random.randint(key_of[2], (2, ROWS), 0, 3), jax.random.fold_in(key_of[2], 1), 0, 2).astype(jnp.int32),
        "pivots": draw_pivots(jax.random.fold_in(key_of[6], 71), 0),
        "lower_inv": draw_lower_inv(jax.random.fold_in(key_of[6], 71), 0),
        "upper_inv": draw_upper_inv(jax.random.fold_in(key_of[6], 71), 0),
    }


wave_number = 2.0 * math.pi
core_square = 0.0025
edge_square = 0.0225
quad_bary = ((1.0 / 3.0, 1.0 / 3.0, 1.0 / 3.0), (0.05971587178977, 0.470142064105115, 0.470142064105115), (0.470142064105115, 0.05971587178977, 0.470142064105115), (0.470142064105115, 0.470142064105115, 0.05971587178977), (0.797426985353087, 0.101286507323456, 0.101286507323456), (0.101286507323456, 0.797426985353087, 0.101286507323456), (0.101286507323456, 0.101286507323456, 0.797426985353087))
quad_weight = (0.225, 0.132394152788506, 0.132394152788506, 0.132394152788506, 0.125939180544827, 0.125939180544827, 0.125939180544827)

def exact_dot(first_matrix, second_matrix):
    return jnp.dot(first_matrix, second_matrix, precision=lax.Precision.HIGHEST)

def complex_dot(first_real, first_imag, second_real, second_imag):
    out_real = exact_dot(first_real, second_real) - exact_dot(first_imag, second_imag)
    out_imag = exact_dot(first_real, second_imag) + exact_dot(first_imag, second_real)
    return (out_real, out_imag)

def triangle_data(corners, free_index):
    total_count = corners.shape[1]
    vertex = corners.reshape(3, 3, total_count)
    choose = (free_index[None, :] == jnp.arange(3, dtype=jnp.int32)[:, None]).astype(corners.dtype)
    free_vertex = lax.optimization_barrier(jnp.sum(choose[:, None, :] * vertex, axis=0))
    after_one = lax.optimization_barrier(jnp.sum(jnp.roll(choose, 1, axis=0)[:, None, :] * vertex, axis=0))
    after_two = lax.optimization_barrier(jnp.sum(jnp.roll(choose, 2, axis=0)[:, None, :] * vertex, axis=0))
    edge_side = after_one - after_two
    length = jnp.sqrt(lax.optimization_barrier(jnp.sum(edge_side * edge_side, axis=0)))
    normal = jnp.cross(vertex[1] - vertex[0], vertex[2] - vertex[0], axis=0)
    tri_area = 0.5 * jnp.sqrt(lax.optimization_barrier(jnp.sum(normal * normal, axis=0)))
    points = jnp.stack([quad_bary[point_index][0] * vertex[0] + quad_bary[point_index][1] * vertex[1] + quad_bary[point_index][2] * vertex[2] for point_index in range(7)], axis=1)
    return (points, free_vertex, length, tri_area)

def edge_geometry(plus_corners, minus_corners, plus_free, minus_free):
    plus_points, plus_vertex, length, plus_area = triangle_data(plus_corners, plus_free)
    minus_points, minus_vertex, spare_length, minus_area = triangle_data(minus_corners, minus_free)
    weight = jnp.array(quad_weight, dtype=plus_area.dtype)[:, None]
    plus_vec = (length / (2.0 * plus_area))[None, None, :] * (plus_points - plus_vertex[:, None, :])
    minus_vec = (length / (2.0 * minus_area))[None, None, :] * (minus_vertex[:, None, :] - minus_points)
    points = jnp.stack([plus_points, minus_points])
    vectors = jnp.stack([plus_vec, minus_vec])
    divergence = jnp.stack([length / plus_area, -length / minus_area])
    weighted = jnp.stack([weight * plus_area[None, :], weight * minus_area[None, :]])
    return (points, vectors, divergence, weighted)

def fill_block(test_geometry, source_geometry):
    test_points, test_vectors, test_div, test_weight = test_geometry
    source_points, source_vectors, source_div, source_weight = source_geometry
    row_count = test_div.shape[1]
    col_count = source_div.shape[1]

    def one_point(point_index, totals):
        real_sum, imag_sum = totals
        for test_sign in range(2):
            here = lax.dynamic_index_in_dim(test_points[test_sign], point_index, 1, keepdims=False)
            along = lax.dynamic_index_in_dim(test_vectors[test_sign], point_index, 1, keepdims=False)
            test_scale = lax.dynamic_index_in_dim(test_weight[test_sign], point_index, 0, keepdims=False)
            for source_sign in range(2):
                there = source_points[source_sign]
                other = source_vectors[source_sign]
                gap_x = here[0][None, :, None] - there[0][:, None, :]
                gap_y = here[1][None, :, None] - there[1][:, None, :]
                gap_z = here[2][None, :, None] - there[2][:, None, :]
                distance = jnp.sqrt(gap_x * gap_x + gap_y * gap_y + gap_z * gap_z + core_square)
                inner_product = along[0][None, :, None] * other[0][:, None, :] + along[1][None, :, None] * other[1][:, None, :] + along[2][None, :, None] * other[2][:, None, :]
                factor = wave_number * inner_product - test_div[test_sign][None, :, None] * source_div[source_sign][None, None, :] / wave_number
                factor = factor * (test_scale[None, :, None] * source_weight[source_sign][:, None, :]) / (edge_square * distance)
                phase_angle = wave_number * distance
                real_sum = real_sum + lax.optimization_barrier(jnp.sum(factor * jnp.sin(phase_angle), axis=0))
                imag_sum = imag_sum + lax.optimization_barrier(jnp.sum(factor * jnp.cos(phase_angle), axis=0))
        return (real_sum, imag_sum)
    empty_sum = jnp.zeros((row_count, col_count), dtype=test_div.dtype)
    return lax.fori_loop(0, 7, one_point, (empty_sum, empty_sum))

def reference(tri_corners, edge_tris, edge_free, pivots, lower_inv, upper_inv):
    geometry = edge_geometry(jnp.take(tri_corners, edge_tris[0], axis=1), jnp.take(tri_corners, edge_tris[1], axis=1), edge_free[0], edge_free[1])
    source_geometry = jax.tree.map(lambda member: member[..., :SLAB], geometry)

    def one_block(block_number):
        first_row = block_number * R_DEV
        test_geometry = jax.tree.map(lambda member: lax.dynamic_slice_in_dim(member, first_row, R_DEV, member.ndim - 1), geometry)
        return fill_block(test_geometry, source_geometry)
    real_part, imag_part = lax.map(one_block, jnp.arange(N_PROW, dtype=jnp.int32))
    real_part = real_part.reshape(ROWS, SLAB)
    imag_part = imag_part.reshape(ROWS, SLAB)
    for panel_number in range(PANELS):
        panel_start = panel_number * PW
        finish = panel_start + PW
        pivot_rows = pivots[panel_number]
        incoming_real = real_part[pivot_rows]
        incoming_imag = imag_part[pivot_rows]
        initial_real = real_part[panel_start:finish]
        initial_imag = imag_part[panel_start:finish]
        real_part = real_part.at[pivot_rows].set(initial_real).at[panel_start:finish].set(incoming_real)
        imag_part = imag_part.at[pivot_rows].set(initial_imag).at[panel_start:finish].set(incoming_imag)
        left_real, left_imag = complex_dot(real_part[finish:, panel_start:finish], imag_part[finish:, panel_start:finish], upper_inv[panel_number, 0], upper_inv[panel_number, 1])
        right_real, right_imag = complex_dot(lower_inv[panel_number, 0], lower_inv[panel_number, 1], incoming_real[:, finish:], incoming_imag[:, finish:])
        update_real, update_imag = complex_dot(left_real, left_imag, right_real, right_imag)
        real_part = real_part.at[finish:, finish:].set(real_part[finish:, finish:] - update_real)
        imag_part = imag_part.at[finish:, finish:].set(imag_part[finish:, finish:] - update_imag)
        real_part = real_part.at[finish:, panel_start:finish].set(left_real)
        imag_part = imag_part.at[finish:, panel_start:finish].set(left_imag)
    per_column = SLAB // N_PCOL
    layout = jnp.stack([real_part.reshape(ROWS, N_PCOL, per_column), imag_part.reshape(ROWS, N_PCOL, per_column)], axis=2)
    return layout.reshape(ROWS, 2 * SLAB)
```

```python
import functools
import math

import jax
import jax.numpy as jnp
import numpy as np
from jax import lax
from jax.experimental import pallas as pl
from jax.experimental.pallas import tpu as pltpu
from jax.sharding import PartitionSpec as P

SLAB = 512
LANES = 128
TILE = 8
F32 = jnp.float32
BF16 = jnp.bfloat16
HIGH = lax.Precision.HIGHEST
PIECES = 4

WAVE = 2.0 * math.pi
CORE = 0.0025
EDGE = 0.0225
W0, W1, W2 = 0.225, 0.132394152788506, 0.125939180544827
A1, C1 = 0.05971587178977, 0.470142064105115
A2, C2 = 0.797426985353087, 0.101286507323456
BARY = np.array(
    [
        (1.0 / 3.0, 1.0 / 3.0, 1.0 / 3.0),
        (A1, C1, C1),
        (C1, A1, C1),
        (C1, C1, A1),
        (A2, C2, C2),
        (C2, A2, C2),
        (C2, C2, A2),
    ]
)
SIN_PI = (4.442882834891847, -7.308241184643747, 3.6062893310962023, -0.8457654013401454, 0.10920875202031989)
COS_PI = (1.4142134965650288, -6.97885098824092, 5.739461170720994, -1.8835629875540871, 0.31069819231686724)
TURN = 12582912.0
POINTS, EDGES, CONST, SIDE = 0, 21, 27, 28
VMEM_WHOLE = pl.BlockSpec(memory_space=pltpu.VMEM)


def horner(coefficients, x):
    total = coefficients[-1] * x + coefficients[-2]
    for value in coefficients[-3::-1]:
        total = total * x + value
    return total


def green(square):
    inverse = lax.rsqrt(square)
    turns = square * inverse
    turns = turns - ((turns + TURN) - TURN)
    power = turns * turns
    half_sin = turns * horner(SIN_PI, power)
    half_cos = horner(COS_PI, power)
    scaled = half_sin * inverse
    return scaled * half_cos, inverse - scaled * half_sin


def total_moment(g):
    return W0 * g[0] + W1 * (g[1] + (g[2] + g[3])) + W2 * (g[4] + (g[5] + g[6]))


def corner_moments(g, corners):
    first, second = g[1] + (g[2] + g[3]), g[4] + (g[5] + g[6])
    base = (W0 / 3.0) * g[0] + (W1 * C1) * first + (W2 * C2) * second
    return [base + (W1 * (A1 - C1)) * g[1 + i] + (W2 * (A2 - C2)) * g[4 + i] for i in corners]


def fill_tile(test_ref, source_ref, rows, lanes):
    shape = (TILE, LANES)
    total = [[None] * 3 for _ in range(2)]

    def source(k):
        return jnp.broadcast_to(source_ref[pl.ds(k, 1), lanes], shape)

    for side in range(2):
        test_rows = test_ref[side, rows, :]

        def test(k):
            return jnp.broadcast_to(test_rows[:, k : k + 1], shape)

        here = [[test(POINTS + 3 * p + c) for c in range(3)] for p in range(7)]
        kept = [[[], [], []], [[], [], []]]
        for q in range(7):
            there = [source(POINTS + 3 * q + c) for c in range(3)]
            values = []
            for p in range(7):
                x, y, z = (here[p][c] - there[c] for c in range(3))
                values.append(green(x * x + (y * y + (z * z + CORE))))
            for part in range(2):
                g = [value[part] for value in values]
                for k, moment in enumerate([total_moment(g)] + corner_moments(g, (1, 2))):
                    kept[part][k].append(moment)
        sides = [[source(EDGES + 3 * e + c) for c in range(3)] for e in range(2)]
        dots = []
        for i in range(2):
            arm = [test(EDGES + 3 * i + c) for c in range(3)]
            one, two = (sum(arm[c] * sides[e][c] for c in range(3)) for e in range(2))
            dots.append((one, two, two - one))
        constant = test(CONST)
        for part in range(2):
            whole = constant * total_moment(kept[part][0])
            moments = [corner_moments(kept[part][1 + i], (0, 1, 2)) for i in range(2)]
            (m10, m11, m12), (m20, m21, m22) = moments
            (a1, a2, a3), (b1, b2, b3) = dots
            found = (
                (m11 * a1 + m12 * a2) + (m21 * b1 + m22 * b2) - whole,
                (m12 * a3 - m10 * a1) + (m22 * b3 - m20 * b1) - whole,
                -(m10 * a2 + m11 * a3) - (m20 * b2 + m21 * b3) - whole,
            )
            for j in range(3):
                total[part][j] = found[j] if side == 0 else total[part][j] + found[j]
    return total


def split_three(value):
    first = value.astype(BF16)
    rest = value - first.astype(F32)
    second = rest.astype(BF16)
    third = (rest - second.astype(F32)).astype(BF16)
    return first, second, third


def dot(a, b):
    return lax.dot_general(a, b, (((1,), (0,)), ((), ())), preferred_element_type=F32)


def dot_exact(a, b):
    return lax.dot_general(a, b, (((1,), (0,)), ((), ())), precision=HIGH, preferred_element_type=F32)


def dot_select(a, b):
    return sum(dot(part, b) for part in split_three(a))


def geometry_matrices():
    out = np.zeros((3, 9, 32))
    for f in range(3):
        order = [(f + i) % 3 for i in range(3)]
        for c in range(3):
            for p in range(7):
                for i in range(3):
                    out[f, 3 * order[i] + c, POINTS + 3 * p + c] = BARY[p, i]
            for e in range(2):
                out[f, 3 * order[1 + e] + c, EDGES + 3 * e + c] = 1.0
                out[f, 3 * order[0] + c, EDGES + 3 * e + c] = -1.0
            out[f, 3 * order[1] + c, SIDE + c] = 1.0
            out[f, 3 * order[2] + c, SIDE + c] = -1.0
    return out


class Sizes:
    def __init__(self, mesh, width, panel):
        self.prow, self.pcol = mesh.shape["prow"], mesh.shape["pcol"]
        self.width = width
        self.block = width * self.pcol
        self.panel = panel
        self.rows = self.block // self.pcol
        self.fold = LANES // width
        self.chunk = TILE
        self.blocks = SLAB // self.block
        self.per_column = SLAB // self.pcol
        self.spread = max(1, min(self.pcol, panel // TILE // self.prow))
        self.pivot_rows = panel // (self.prow * self.spread)

    def by_slot(self, matrix):
        out = np.zeros((self.fold, TILE, matrix.shape[1]), np.float32)
        for q in range(9):
            out[q % self.fold, q // self.fold] = matrix[q]
        return out


def pack_kernel(size, corner_ref, tris_ref, free_ref, out_ref):
    col = lax.axis_index("pcol")
    width = size.width
    tables = jnp.concatenate([tris_ref[...], free_ref[...]], axis=0).astype(F32)
    here = jnp.zeros((4, width), F32)
    for part in range(size.pcol):
        here = jnp.where(col == part, tables[:, part * width : (part + 1) * width], here)
    rows = [corner_ref[q : q + 1, :] for q in range(9)] + [here[q : q + 1, :] for q in range(4)]
    blank = jnp.zeros((1, width), F32)
    rows = rows + [blank] * (TILE * size.fold - len(rows))
    lines = [jnp.concatenate(rows[k * size.fold : (k + 1) * size.fold], axis=1) for k in range(TILE)]
    chunk = jnp.concatenate(lines, axis=0)
    out_ref[...] = jnp.broadcast_to(chunk[None], out_ref.shape)


def prepare_kernel(
    size, packed_ref, pivot_ref, test_map_ref, source_map_ref,
    test_ref, source_ref, select_ref, length_ref, incoming_ref, mine_ref, moment_ref,
):
    row, col = lax.axis_index("prow"), lax.axis_index("pcol")
    devices = size.prow * size.pcol
    fold, width, block = size.fold, size.width, size.block
    count = size.rows + size.pivot_rows

    line = lax.broadcasted_iota(jnp.int32, (count, 1), 0)
    part = row * size.spread + lax.rem(col, size.spread)
    mine = jnp.where(
        line < size.rows,
        row * block + col * size.rows + line,
        part * size.pivot_rows + (line - size.rows),
    )
    pivots = jnp.broadcast_to(pivot_ref[...], (count, size.panel))
    slots = lax.broadcasted_iota(jnp.int32, (count, size.panel), 1)
    brought = jnp.sum(jnp.where(slots == mine, pivots, 0).astype(F32), axis=1, keepdims=True)
    moved = pivots == mine
    displaced = jnp.sum(jnp.where(moved, slots, 0).astype(F32), axis=1, keepdims=True)
    was_moved = jnp.sum(jnp.where(moved, 1.0, 0.0), axis=1, keepdims=True) > 0.5
    edge = jnp.where(
        mine < size.panel, brought, jnp.where(was_moved, displaced, mine.astype(F32))
    ).astype(jnp.int32)

    step = 32

    def look_up(index):
        place = (index // width) * LANES + lax.rem(index, width)
        number = index.shape[0]

        def one(k, sums):
            base = pl.multiple_of(k * (step * TILE), step * TILE)
            block_rows = packed_ref[pl.ds(base, step * TILE), :]
            flat = jnp.concatenate(
                [block_rows[d * TILE : (d + 1) * TILE] for d in range(step)], axis=1
            )
            parts = split_three(flat)
            lane = lax.broadcasted_iota(jnp.int32, (number, step * LANES), 1) + k * (step * LANES)
            out = []
            for s in range(fold):
                hot = jnp.where(lane == place + s * width, 1.0, 0.0).astype(BF16)
                found = sums[s]
                for piece in parts:
                    found = found + lax.dot_general(
                        hot, piece, (((1,), (1,)), ((), ())), preferred_element_type=F32
                    )
                out.append(found)
            return tuple(out)

        start = tuple(jnp.zeros((number, TILE), F32) for _ in range(fold))
        if devices == step:
            return one(0, start)
        return lax.fori_loop(0, devices // step, one, start)

    def column(slots_found, q):
        return slots_found[q % fold][:, q // fold : q // fold + 1]

    tables = look_up(edge)
    triangle = jnp.concatenate([column(tables, 9), column(tables, 10)], axis=0).astype(jnp.int32)
    free = jnp.concatenate([column(tables, 11), column(tables, 12)], axis=0)
    corners = look_up(triangle)
    test = jnp.zeros((2 * count, 32), F32)
    for f in range(3):
        made = sum(dot_exact(corners[s], test_map_ref[f, s]) for s in range(fold))
        test = jnp.where(free == float(f), made, test)
    lane = lax.broadcasted_iota(jnp.int32, (2 * count, 32), 1)
    side = jnp.where((lane >= SIDE) & (lane < SIDE + 3), test, 0.0)
    length = jnp.sqrt(jnp.sum(side * side, axis=1, keepdims=True))[:count]
    length = jnp.concatenate([length, -length], axis=0) / EDGE
    scale = jnp.where(lane < EDGES, 1.0, length * (WAVE / 4.0))
    test = jnp.where(lane == CONST, length / WAVE, test * scale)
    for s in range(2):
        test_ref[s] = test[s * count : s * count + size.rows]
        mine_ref[s] = test[s * count + size.rows : (s + 1) * count]

    lane = lax.broadcasted_iota(jnp.int32, (TILE, LANES), 1)
    by_slot = [[] for _ in range(fold)]
    for t in range(SLAB // LANES):
        pieces = [packed_ref[(t * fold + i) * TILE : (t * fold + i + 1) * TILE, :] for i in range(fold)]
        for s in range(fold):
            found = jnp.zeros((TILE, LANES), F32)
            for i in range(fold):
                shift = ((i - s) * width) % LANES
                turned = pltpu.roll(pieces[i], shift, 1) if shift else pieces[i]
                found = jnp.where((lane >= i * width) & (lane < (i + 1) * width), turned, found)
            by_slot[s].append(found)
    by_slot = [jnp.concatenate(found, axis=1) for found in by_slot]
    source = sum(dot_exact(source_map_ref[s], by_slot[s]) for s in range(fold))
    source_ref[...] = source
    one, two = source[EDGES : EDGES + 3], source[EDGES + 3 : EDGES + 6]
    third = two - one
    lengths = [jnp.sqrt(jnp.sum(v * v, axis=0, keepdims=True)) for v in (third, two, one)]

    def quantity(q):
        return by_slot[q % fold][q // fold : q // fold + 1, :]

    place = lax.broadcasted_iota(jnp.int32, (3 * block, block), 0)
    for b in range(size.blocks):
        cols = slice(b * block, (b + 1) * block)
        code = []
        for sign in range(2):
            local = quantity(9 + sign)[:, cols] - float(b * block)
            code.append((local + quantity(11 + sign)[:, cols] * float(block)).astype(jnp.int32))
        plus = jnp.where(place == code[0], 1.0, 0.0)
        minus = jnp.where(place == code[1], 1.0, 0.0)
        line = jnp.concatenate([v[:, cols] for v in lengths], axis=1)
        line = jnp.broadcast_to(line, (TILE, 3 * block))
        length_ref[:, cols] = dot_select(line, plus.astype(BF16))
        select_ref[b] = (plus - minus).astype(BF16)

    last = size.blocks - 1

    def tile(t, carry):
        lanes = pl.ds(pl.multiple_of(t * LANES + last * block, LANES), LANES)
        total = fill_tile(mine_ref, source_ref, pl.ds(0, TILE), lanes)
        for p in range(2):
            for j in range(3):
                target = pl.ds(pl.multiple_of(j * block + t * LANES, LANES), LANES)
                moment_ref[p * TILE : (p + 1) * TILE, target] = total[p][j]
        return carry

    lax.fori_loop(0, block // LANES, tile, 0)
    made = dot_select(moment_ref[...], select_ref[last])
    made = made * length_ref[0:1, last * block : (last + 1) * block]
    incoming_ref[:, :block] = made[:TILE]
    incoming_ref[:, block:] = made[TILE:]


def fill_kernel(size, piece, pieces, test_ref, source_ref, moment_ref):
    tiles = size.rows // TILE
    across = SLAB // LANES
    here = tiles * across // pieces

    def body(step, carry):
        t = piece * here + step
        lt = lax.rem(t, across)
        row = pl.multiple_of((t // across) * TILE, TILE)
        lane = pl.multiple_of(lt * LANES, LANES)
        out = pl.ds(pl.multiple_of((step // across) * TILE, TILE), TILE)
        total = fill_tile(test_ref, source_ref, pl.ds(row, TILE), pl.ds(lane, LANES))
        for p in range(2):
            for j in range(3):
                moment_ref[p, j, out, pl.ds(lane, LANES)] = total[p][j]
        return carry

    lax.fori_loop(0, here, body, 0)


def finish_kernel(size, parts, order_lu, order_in, *refs):
    moments = refs[:parts]
    select_ref, length_ref, lu_a, lu_b, in_a, in_b, out_ref, lower_ref, upper_ref, pivot_ref = refs[parts:]
    row, col = lax.axis_index("prow"), lax.axis_index("pcol")
    block, rows, panel = size.block, size.rows, size.panel
    each = panel // size.prow

    half = len(order_lu) // 2
    for k, flip in enumerate(order_lu):
        ref, slot = (lu_a, k) if k < half else (lu_b, k - half)
        owner = pl.multiple_of((row ^ flip) * each, each)
        for m, target in enumerate((lower_ref, upper_ref)):
            for p in range(2):
                start = (slot * 4 + 2 * m + p) * each
                target[p, pl.ds(owner, each), :] = ref[start : start + each, :]
    half = len(order_in) // 2
    for k, (flip_row, flip_col) in enumerate(order_in):
        ref, slot = (in_a, k) if k < half else (in_b, k - half)
        part = (row ^ flip_row) * size.spread + lax.rem(col ^ flip_col, size.spread)
        owner = pl.multiple_of(part * size.pivot_rows, size.pivot_rows)
        start = slot * size.pivot_rows
        pivot_ref[pl.ds(owner, size.pivot_rows), :] = ref[start : start + size.pivot_rows, :]

    def assemble(b):
        cols = slice(b * block, (b + 1) * block)
        lines = []
        for p in range(2):
            joined = [
                jnp.concatenate([m[p, j, :, cols] for j in range(3)], axis=1) for m in moments
            ]
            lines.append(jnp.concatenate(joined, axis=0))
        made = dot_select(jnp.concatenate(lines, axis=0), select_ref[b])
        made = made * length_ref[0:1, cols]
        return made[:rows], made[rows:]

    def complex_dot(a, b):
        both = jnp.concatenate([a[0], a[1]], axis=0)
        count = a[0].shape[0]
        first, second = dot_exact(both, b[0]), dot_exact(both, b[1])
        return first[:count] - second[count:], second[:count] + first[count:]

    left = assemble(0)
    trailing = assemble(1)
    right = complex_dot((lower_ref[0], lower_ref[1]), (pivot_ref[:, :block], pivot_ref[:, block:]))
    factor = complex_dot(left, (upper_ref[0], upper_ref[1]))
    update = complex_dot(factor, right)
    line = row * block + col * rows + lax.broadcasted_iota(jnp.int32, (rows, block), 0)
    below = line >= panel
    width = size.per_column
    for p in range(2):
        panel_out = jnp.where(below, factor[p], left[p])
        trailing_out = jnp.where(below, trailing[p] - update[p], trailing[p])
        both = jnp.concatenate([panel_out, trailing_out], axis=1)
        for c in range(size.pcol):
            out_ref[c, :, p * width : (p + 1) * width] = both[:, c * width : (c + 1) * width]


def bits(count):
    return [1 << b for b in reversed(range(count.bit_length() - 1))]


def per_device(size, tri_corners, edge_tris, edge_free, pivots, lower_inv, upper_inv):
    prow, pcol = size.prow, size.pcol
    devices = prow * pcol
    call = functools.partial(pl.pallas_call)

    def struct(*shape, dtype=F32):
        return jax.ShapeDtypeStruct(shape, dtype)

    def cost(us):
        return pl.CostEstimate(flops=int(us * 1e9), bytes_accessed=1024, transcendentals=0)

    each = size.panel // prow
    lu = jnp.concatenate(
        [lower_inv.reshape(2 * each, size.panel), upper_inv.reshape(2 * each, size.panel)], axis=0
    )
    lu_order = [0]
    lu_steps = bits(prow)
    lu_other = None
    for n, bit in enumerate(lu_steps):
        if n:
            lu = jnp.concatenate([lu, lu_other], axis=0)
        lu_other = lax.ppermute(lu, "prow", [(i, i ^ bit) for i in range(prow)])
        lu_order = lu_order + [o ^ bit for o in lu_order]

    packed = call(
        functools.partial(pack_kernel, size),
        out_shape=struct(devices, TILE, LANES),
        in_specs=[VMEM_WHOLE] * 3,
        out_specs=VMEM_WHOLE,
        name="pack_geometry",
    )(tri_corners, edge_tris, edge_free)
    packed = lax.all_to_all(packed.reshape(devices * TILE, LANES), ("prow", "pcol"), 0, 0, tiled=True)

    maps = geometry_matrices()
    test_map = jnp.asarray(np.stack([size.by_slot(maps[f]) for f in range(3)]), F32)
    source_map = jnp.asarray(np.transpose(size.by_slot(maps[0]), (0, 2, 1)), F32)
    last = size.blocks - 1
    test, source, select, length, incoming = call(
        functools.partial(prepare_kernel, size),
        out_shape=(
            struct(2, size.rows, 32),
            struct(32, SLAB),
            struct(size.blocks, 3 * size.block, size.block, dtype=BF16),
            struct(TILE, SLAB),
            struct(size.pivot_rows, 2 * size.block),
        ),
        in_specs=[VMEM_WHOLE] * 4,
        out_specs=(VMEM_WHOLE,) * 5,
        scratch_shapes=[
            pltpu.VMEM((2, size.pivot_rows, 32), F32),
            pltpu.VMEM((2 * TILE, 3 * size.block), F32),
        ],
        cost_estimate=cost(5),
        name="prepare_slab",
    )(packed, pivots, test_map, source_map)

    tiles = size.rows // TILE
    pieces = min(PIECES, tiles)
    moments = []
    for piece in range(pieces):
        moments.append(
            call(
                functools.partial(fill_kernel, size, piece, pieces),
                out_shape=struct(2, 3, size.rows // pieces, SLAB),
                in_specs=[VMEM_WHOLE] * 2,
                out_specs=VMEM_WHOLE,
                cost_estimate=cost(24 / pieces),
                name=f"fill_slab_{piece}",
            )(test, source)
        )

    order = [(0, 0)]
    row_bits = bits(prow)
    steps = [("prow", b) for b in row_bits[:-1]] + [("pcol", b) for b in reversed(bits(size.spread))]
    steps = steps + [("prow", b) for b in row_bits[-1:]]
    other = None
    for n, (axis, bit) in enumerate(steps):
        if n:
            incoming = jnp.concatenate([incoming, other], axis=0)
        count = prow if axis == "prow" else pcol
        other = lax.ppermute(incoming, axis, [(i, i ^ bit) for i in range(count)])
        order = order + [
            (a ^ bit, b) if axis == "prow" else (a, b ^ bit) for a, b in order
        ]

    tile = call(
        functools.partial(finish_kernel, size, pieces, lu_order, order),
        out_shape=struct(pcol, size.rows, 2 * size.per_column),
        in_specs=[VMEM_WHOLE] * (pieces + 6),
        out_specs=VMEM_WHOLE,
        scratch_shapes=[
            pltpu.VMEM((2, size.panel, size.panel), F32),
            pltpu.VMEM((2, size.panel, size.panel), F32),
            pltpu.VMEM((size.panel, 2 * size.block), F32),
        ],
        cost_estimate=cost(4),
        name="finish_slab",
    )(*moments, select, length, lu, lu_other, incoming, other)
    tile = tile.reshape(pcol * size.rows, 2 * size.per_column)
    return lax.all_to_all(tile, "pcol", 0, 0, tiled=True)


def solution(mesh):
    in_specs = (
        P(None, ("prow", "pcol")),
        P(None, "prow"),
        P(None, "prow"),
        P(),
        P(None, None, "prow", None),
        P(None, None, "prow", None),
    )

    def body(tri_corners, edge_tris, edge_free, pivots, lower_inv, upper_inv):
        size = Sizes(mesh, tri_corners.shape[1], pivots.shape[1])
        return per_device(size, tri_corners, edge_tris, edge_free, pivots, lower_inv, upper_inv)

    return jax.shard_map(
        body, mesh=mesh, in_specs=in_specs, out_specs=P("prow", "pcol"), check_vma=False
    )
```

```python
import functools
import math

import jax
import jax.numpy as jnp
import numpy as np
from jax import lax
from jax.experimental import pallas as pl
from jax.experimental.pallas import tpu as pltpu
from jax.sharding import PartitionSpec as P

SLAB = 512
LANES = 128
TILE = 8
F32 = jnp.float32
BF16 = jnp.bfloat16
HIGH = lax.Precision.HIGHEST
SMALL = 4 << 20
LARGE = 16 << 20

WAVE = 2.0 * math.pi
CORE = 0.0025
EDGE = 0.0225
W0, W1, W2 = 0.225, 0.132394152788506, 0.125939180544827
A1, C1 = 0.05971587178977, 0.470142064105115
A2, C2 = 0.797426985353087, 0.101286507323456
BARY = np.array(
    [
        (1.0 / 3.0, 1.0 / 3.0, 1.0 / 3.0),
        (A1, C1, C1),
        (C1, A1, C1),
        (C1, C1, A1),
        (A2, C2, C2),
        (C2, A2, C2),
        (C2, C2, A2),
    ]
)
SIN_PI = (4.442882834891847, -7.308241184643747, 3.6062893310962023, -0.8457654013401454, 0.10920875202031989)
COS_PI = (1.4142134965650288, -6.97885098824092, 5.739461170720994, -1.8835629875540871, 0.31069819231686724)
TURN = 12582912.0
POINTS, EDGES, CONST, SIDE = 0, 21, 27, 28
VMEM_WHOLE = pl.BlockSpec(memory_space=pltpu.VMEM)


def horner(coefficients, x):
    total = coefficients[-1] * x + coefficients[-2]
    for value in coefficients[-3::-1]:
        total = total * x + value
    return total


def green(square):
    inverse = lax.rsqrt(square)
    turns = square * inverse
    turns = turns - ((turns + TURN) - TURN)
    power = turns * turns
    half_sin = turns * horner(SIN_PI, power)
    half_cos = horner(COS_PI, power)
    scaled = half_sin * inverse
    return scaled * half_cos, inverse - scaled * half_sin


def total_moment(g):
    return W0 * g[0] + W1 * (g[1] + (g[2] + g[3])) + W2 * (g[4] + (g[5] + g[6]))


def corner_moments(g, corners):
    first, second = g[1] + (g[2] + g[3]), g[4] + (g[5] + g[6])
    base = (W0 / 3.0) * g[0] + (W1 * C1) * first + (W2 * C2) * second
    return [base + (W1 * (A1 - C1)) * g[1 + i] + (W2 * (A2 - C2)) * g[4 + i] for i in corners]


def fill_tile(test_ref, source_ref, rows, lanes):
    shape = (TILE, LANES)
    total = [[None] * 3 for _ in range(2)]

    def source(k):
        return jnp.broadcast_to(source_ref[pl.ds(k, 1), lanes], shape)

    for side in range(2):
        test_rows = test_ref[side, rows, :]

        def test(k):
            return jnp.broadcast_to(test_rows[:, k : k + 1], shape)

        here = [[test(POINTS + 3 * p + c) for c in range(3)] for p in range(7)]
        kept = [[[], [], []], [[], [], []]]
        for q in range(7):
            there = [source(POINTS + 3 * q + c) for c in range(3)]
            values = []
            for p in range(7):
                x, y, z = (here[p][c] - there[c] for c in range(3))
                values.append(green(x * x + (y * y + (z * z + CORE))))
            for part in range(2):
                g = [value[part] for value in values]
                for k, moment in enumerate([total_moment(g)] + corner_moments(g, (1, 2))):
                    kept[part][k].append(moment)
        sides = [[source(EDGES + 3 * e + c) for c in range(3)] for e in range(2)]
        dots = []
        for i in range(2):
            arm = [test(EDGES + 3 * i + c) for c in range(3)]
            one, two = (sum(arm[c] * sides[e][c] for c in range(3)) for e in range(2))
            dots.append((one, two, two - one))
        constant = test(CONST)
        for part in range(2):
            whole = constant * total_moment(kept[part][0])
            moments = [corner_moments(kept[part][1 + i], (0, 1, 2)) for i in range(2)]
            (m10, m11, m12), (m20, m21, m22) = moments
            (a1, a2, a3), (b1, b2, b3) = dots
            found = (
                (m11 * a1 + m12 * a2) + (m21 * b1 + m22 * b2) - whole,
                (m12 * a3 - m10 * a1) + (m22 * b3 - m20 * b1) - whole,
                -(m10 * a2 + m11 * a3) - (m20 * b2 + m21 * b3) - whole,
            )
            for j in range(3):
                total[part][j] = found[j] if side == 0 else total[part][j] + found[j]
    return total


def split_three(value):
    first = value.astype(BF16)
    rest = value - first.astype(F32)
    second = rest.astype(BF16)
    third = (rest - second.astype(F32)).astype(BF16)
    return first, second, third


def dot(a, b):
    return lax.dot_general(a, b, (((1,), (0,)), ((), ())), preferred_element_type=F32)


def dot_exact(a, b):
    return lax.dot_general(a, b, (((1,), (0,)), ((), ())), precision=HIGH, preferred_element_type=F32)


def dot_select(a, b):
    return sum(dot(part, b) for part in split_three(a))


def geometry_matrices():
    out = np.zeros((3, 9, 32))
    for f in range(3):
        order = [(f + i) % 3 for i in range(3)]
        for c in range(3):
            for p in range(7):
                for i in range(3):
                    out[f, 3 * order[i] + c, POINTS + 3 * p + c] = BARY[p, i]
            for e in range(2):
                out[f, 3 * order[1 + e] + c, EDGES + 3 * e + c] = 1.0
                out[f, 3 * order[0] + c, EDGES + 3 * e + c] = -1.0
            out[f, 3 * order[1] + c, SIDE + c] = 1.0
            out[f, 3 * order[2] + c, SIDE + c] = -1.0
    return out


class Sizes:
    def __init__(self, mesh, width, panel):
        self.prow, self.pcol = mesh.shape["prow"], mesh.shape["pcol"]
        self.width = width
        self.block = width * self.pcol
        self.panel = panel
        self.rows = self.block // self.pcol
        self.fold = LANES // width
        self.chunk = TILE
        self.blocks = SLAB // self.block
        self.per_column = SLAB // self.pcol
        self.spread = max(1, min(self.pcol, panel // TILE // self.prow))
        self.pivot_rows = panel // (self.prow * self.spread)

    def by_slot(self, matrix):
        out = np.zeros((self.fold, TILE, matrix.shape[1]), np.float32)
        for q in range(9):
            out[q % self.fold, q // self.fold] = matrix[q]
        return out


def pack_kernel(size, corner_ref, tris_ref, free_ref, out_ref):
    col = lax.axis_index("pcol")
    width = size.width
    tables = jnp.concatenate([tris_ref[...], free_ref[...]], axis=0).astype(F32)
    here = jnp.zeros((4, width), F32)
    for part in range(size.pcol):
        here = jnp.where(col == part, tables[:, part * width : (part + 1) * width], here)
    rows = [corner_ref[q : q + 1, :] for q in range(9)] + [here[q : q + 1, :] for q in range(4)]
    blank = jnp.zeros((1, width), F32)
    rows = rows + [blank] * (TILE * size.fold - len(rows))
    lines = [jnp.concatenate(rows[k * size.fold : (k + 1) * size.fold], axis=1) for k in range(TILE)]
    chunk = jnp.concatenate(lines, axis=0)
    out_ref[...] = jnp.broadcast_to(chunk[None], out_ref.shape)


def prepare_kernel(
    size, packed_ref, pivot_ref, test_map_ref, source_map_ref,
    test_ref, source_ref, select_ref, length_ref, incoming_ref, mine_ref, moment_ref,
):
    row, col = lax.axis_index("prow"), lax.axis_index("pcol")
    devices = size.prow * size.pcol
    fold, width, block = size.fold, size.width, size.block
    count = size.rows + size.pivot_rows

    line = lax.broadcasted_iota(jnp.int32, (count, 1), 0)
    part = row * size.spread + lax.rem(col, size.spread)
    mine = jnp.where(
        line < size.rows,
        row * block + col * size.rows + line,
        part * size.pivot_rows + (line - size.rows),
    )
    pivots = jnp.broadcast_to(pivot_ref[...], (count, size.panel))
    slots = lax.broadcasted_iota(jnp.int32, (count, size.panel), 1)
    brought = jnp.sum(jnp.where(slots == mine, pivots, 0).astype(F32), axis=1, keepdims=True)
    moved = pivots == mine
    displaced = jnp.sum(jnp.where(moved, slots, 0).astype(F32), axis=1, keepdims=True)
    was_moved = jnp.sum(jnp.where(moved, 1.0, 0.0), axis=1, keepdims=True) > 0.5
    edge = jnp.where(
        mine < size.panel, brought, jnp.where(was_moved, displaced, mine.astype(F32))
    ).astype(jnp.int32)

    step = 32

    def look_up(index):
        place = (index // width) * LANES + lax.rem(index, width)
        number = index.shape[0]

        def one(k, sums):
            base = pl.multiple_of(k * (step * TILE), step * TILE)
            block_rows = packed_ref[pl.ds(base, step * TILE), :]
            flat = jnp.concatenate(
                [block_rows[d * TILE : (d + 1) * TILE] for d in range(step)], axis=1
            )
            parts = split_three(flat)
            lane = lax.broadcasted_iota(jnp.int32, (number, step * LANES), 1) + k * (step * LANES)
            out = []
            for s in range(fold):
                hot = jnp.where(lane == place + s * width, 1.0, 0.0).astype(BF16)
                found = sums[s]
                for piece in parts:
                    found = found + lax.dot_general(
                        hot, piece, (((1,), (1,)), ((), ())), preferred_element_type=F32
                    )
                out.append(found)
            return tuple(out)

        start = tuple(jnp.zeros((number, TILE), F32) for _ in range(fold))
        if devices == step:
            return one(0, start)
        return lax.fori_loop(0, devices // step, one, start)

    def column(slots_found, q):
        return slots_found[q % fold][:, q // fold : q // fold + 1]

    tables = look_up(edge)
    triangle = jnp.concatenate([column(tables, 9), column(tables, 10)], axis=0).astype(jnp.int32)
    free = jnp.concatenate([column(tables, 11), column(tables, 12)], axis=0)
    corners = look_up(triangle)
    test = jnp.zeros((2 * count, 32), F32)
    for f in range(3):
        made = sum(dot_exact(corners[s], test_map_ref[f, s]) for s in range(fold))
        test = jnp.where(free == float(f), made, test)
    lane = lax.broadcasted_iota(jnp.int32, (2 * count, 32), 1)
    side = jnp.where((lane >= SIDE) & (lane < SIDE + 3), test, 0.0)
    length = jnp.sqrt(jnp.sum(side * side, axis=1, keepdims=True))[:count]
    length = jnp.concatenate([length, -length], axis=0) / EDGE
    scale = jnp.where(lane < EDGES, 1.0, length * (WAVE / 4.0))
    test = jnp.where(lane == CONST, length / WAVE, test * scale)
    for s in range(2):
        test_ref[s] = test[s * count : s * count + size.rows]
        mine_ref[s] = test[s * count + size.rows : (s + 1) * count]

    lane = lax.broadcasted_iota(jnp.int32, (TILE, LANES), 1)
    by_slot = [[] for _ in range(fold)]
    for t in range(SLAB // LANES):
        pieces = [packed_ref[(t * fold + i) * TILE : (t * fold + i + 1) * TILE, :] for i in range(fold)]
        for s in range(fold):
            found = jnp.zeros((TILE, LANES), F32)
            for i in range(fold):
                shift = ((i - s) * width) % LANES
                turned = pltpu.roll(pieces[i], shift, 1) if shift else pieces[i]
                found = jnp.where((lane >= i * width) & (lane < (i + 1) * width), turned, found)
            by_slot[s].append(found)
    by_slot = [jnp.concatenate(found, axis=1) for found in by_slot]
    source = sum(dot_exact(source_map_ref[s], by_slot[s]) for s in range(fold))
    source_ref[...] = source
    one, two = source[EDGES : EDGES + 3], source[EDGES + 3 : EDGES + 6]
    third = two - one
    lengths = [jnp.sqrt(jnp.sum(v * v, axis=0, keepdims=True)) for v in (third, two, one)]

    def quantity(q):
        return by_slot[q % fold][q // fold : q // fold + 1, :]

    place = lax.broadcasted_iota(jnp.int32, (3 * block, block), 0)
    for b in range(size.blocks):
        cols = slice(b * block, (b + 1) * block)
        code = []
        for sign in range(2):
            local = quantity(9 + sign)[:, cols] - float(b * block)
            code.append((local + quantity(11 + sign)[:, cols] * float(block)).astype(jnp.int32))
        plus = jnp.where(place == code[0], 1.0, 0.0)
        minus = jnp.where(place == code[1], 1.0, 0.0)
        line = jnp.concatenate([v[:, cols] for v in lengths], axis=1)
        line = jnp.broadcast_to(line, (TILE, 3 * block))
        length_ref[:, cols] = dot_select(line, plus.astype(BF16))
        select_ref[b] = (plus - minus).astype(BF16)

    last = size.blocks - 1

    def tile(t, carry):
        lanes = pl.ds(pl.multiple_of(t * LANES + last * block, LANES), LANES)
        total = fill_tile(mine_ref, source_ref, pl.ds(0, TILE), lanes)
        for p in range(2):
            for j in range(3):
                target = pl.ds(pl.multiple_of(j * block + t * LANES, LANES), LANES)
                moment_ref[p * TILE : (p + 1) * TILE, target] = total[p][j]
        return carry

    lax.fori_loop(0, block // LANES, tile, 0)
    made = dot_select(moment_ref[...], select_ref[last])
    made = made * length_ref[0:1, last * block : (last + 1) * block]
    incoming_ref[:, :block] = made[:TILE]
    incoming_ref[:, block:] = made[TILE:]


def fill_kernel(size, first, test_ref, source_ref, moment_ref):
    across = SLAB // LANES
    here = (moment_ref.shape[2] // TILE) * across

    def body(step, carry):
        lt = lax.rem(step, across)
        row = pl.multiple_of((first + step // across) * TILE, TILE)
        lane = pl.multiple_of(lt * LANES, LANES)
        out = pl.ds(pl.multiple_of((step // across) * TILE, TILE), TILE)
        total = fill_tile(test_ref, source_ref, pl.ds(row, TILE), pl.ds(lane, LANES))
        for p in range(2):
            for j in range(3):
                moment_ref[p, j, out, pl.ds(lane, LANES)] = total[p][j]
        return carry

    lax.fori_loop(0, here, body, 0)


def finish_kernel(size, parts, order_lu, order_in, *refs):
    moments = refs[:parts]
    select_ref, length_ref, lu_a, lu_b, in_a, in_b, out_ref, lower_ref, upper_ref, pivot_ref = refs[parts:]
    row, col = lax.axis_index("prow"), lax.axis_index("pcol")
    block, rows, panel = size.block, size.rows, size.panel
    each = panel // size.prow

    half = len(order_lu) // 2
    for k, (flip, _) in enumerate(order_lu):
        ref, slot = (lu_a, k) if k < half else (lu_b, k - half)
        owner = pl.multiple_of((row ^ flip) * each, each)
        for m, target in enumerate((lower_ref, upper_ref)):
            for p in range(2):
                start = (slot * 4 + 2 * m + p) * each
                target[p, pl.ds(owner, each), :] = ref[start : start + each, :]
    half = len(order_in) // 2
    for k, (flip_row, flip_col) in enumerate(order_in):
        ref, slot = (in_a, k) if k < half else (in_b, k - half)
        part = (row ^ flip_row) * size.spread + lax.rem(col ^ flip_col, size.spread)
        owner = pl.multiple_of(part * size.pivot_rows, size.pivot_rows)
        start = slot * size.pivot_rows
        pivot_ref[pl.ds(owner, size.pivot_rows), :] = ref[start : start + size.pivot_rows, :]

    def assemble(b):
        cols = slice(b * block, (b + 1) * block)
        lines = []
        for p in range(2):
            joined = [
                jnp.concatenate([m[p, j, :, cols] for j in range(3)], axis=1) for m in moments
            ]
            lines.append(jnp.concatenate(joined, axis=0))
        made = dot_select(jnp.concatenate(lines, axis=0), select_ref[b])
        made = made * length_ref[0:1, cols]
        return made[:rows], made[rows:]

    def complex_dot(a, b):
        both = jnp.concatenate([a[0], a[1]], axis=0)
        count = a[0].shape[0]
        first, second = dot_exact(both, b[0]), dot_exact(both, b[1])
        return first[:count] - second[count:], second[:count] + first[count:]

    left = assemble(0)
    trailing = assemble(1)
    right = complex_dot((lower_ref[0], lower_ref[1]), (pivot_ref[:, :block], pivot_ref[:, block:]))
    factor = complex_dot(left, (upper_ref[0], upper_ref[1]))
    update = complex_dot(factor, right)
    line = row * block + col * rows + lax.broadcasted_iota(jnp.int32, (rows, block), 0)
    below = line >= panel
    width = size.per_column
    for p in range(2):
        panel_out = jnp.where(below, factor[p], left[p])
        trailing_out = jnp.where(below, trailing[p] - update[p], trailing[p])
        both = jnp.concatenate([panel_out, trailing_out], axis=1)
        for c in range(size.pcol):
            out_ref[c, :, p * width : (p + 1) * width] = both[:, c * width : (c + 1) * width]


class Doubling:
    def __init__(self, held, mesh_sizes, steps):
        self.held, self.other = held, None
        self.sizes, self.steps, self.order = mesh_sizes, list(steps), [(0, 0)]

    def left(self):
        return bool(self.steps)

    def start(self):
        if not self.steps:
            return
        axis, bit = self.steps.pop(0)
        if self.other is not None:
            self.held = jnp.concatenate([self.held, self.other], axis=0)
        pairs = [(i, i ^ bit) for i in range(self.sizes[axis])]
        self.other = lax.ppermute(self.held, axis, pairs)
        self.order = self.order + [
            (a ^ bit, b) if axis == "prow" else (a, b ^ bit) for a, b in self.order
        ]

    def settle(self, after):
        after, self.other = lax.optimization_barrier((after, self.other))
        return after


def bits(count):
    return [1 << b for b in reversed(range(count.bit_length() - 1))]


def per_device(size, tri_corners, edge_tris, edge_free, pivots, lower_inv, upper_inv):
    prow, pcol = size.prow, size.pcol
    devices = prow * pcol
    call = functools.partial(pl.pallas_call)

    def struct(*shape, dtype=F32):
        return jax.ShapeDtypeStruct(shape, dtype)

    def cost(us):
        return pl.CostEstimate(flops=int(us * 1e9), bytes_accessed=1024, transcendentals=0)

    packed = call(
        functools.partial(pack_kernel, size),
        out_shape=struct(devices, TILE, LANES),
        in_specs=[VMEM_WHOLE] * 3,
        out_specs=VMEM_WHOLE,
        compiler_params=pltpu.CompilerParams(vmem_limit_bytes=SMALL),
        name="pack_geometry",
    )(tri_corners, edge_tris, edge_free)
    packed = lax.all_to_all(packed.reshape(devices * TILE, LANES), ("prow", "pcol"), 0, 0, tiled=True)

    each = size.panel // prow
    lower_part, upper_part, packed = lax.optimization_barrier((lower_inv, upper_inv, packed))
    lu = Doubling(
        jnp.concatenate(
            [lower_part.reshape(2 * each, size.panel), upper_part.reshape(2 * each, size.panel)],
            axis=0,
        ),
        mesh_sizes={"prow": prow, "pcol": pcol},
        steps=[("prow", b) for b in bits(prow)],
    )
    lu.start()

    maps = geometry_matrices()
    test_map = jnp.asarray(np.stack([size.by_slot(maps[f]) for f in range(3)]), F32)
    source_map = jnp.asarray(np.transpose(size.by_slot(maps[0]), (0, 2, 1)), F32)
    test, source, select, length, incoming = call(
        functools.partial(prepare_kernel, size),
        out_shape=(
            struct(2, size.rows, 32),
            struct(32, SLAB),
            struct(size.blocks, 3 * size.block, size.block, dtype=BF16),
            struct(TILE, SLAB),
            struct(size.pivot_rows, 2 * size.block),
        ),
        in_specs=[VMEM_WHOLE] * 4,
        out_specs=(VMEM_WHOLE,) * 5,
        scratch_shapes=[
            pltpu.VMEM((2, size.pivot_rows, 32), F32),
            pltpu.VMEM((2 * TILE, 3 * size.block), F32),
        ],
        cost_estimate=cost(5),
        compiler_params=pltpu.CompilerParams(vmem_limit_bytes=LARGE),
        name="prepare_slab",
    )(packed, pivots, test_map, source_map)

    row_bits = bits(prow)
    steps = [("prow", b) for b in row_bits[:-1]] + [("pcol", b) for b in reversed(bits(size.spread))]
    steps = steps + [("prow", b) for b in row_bits[-1:]]
    test = lu.settle(test)
    pivot = Doubling(incoming, mesh_sizes={"prow": prow, "pcol": pcol}, steps=steps)
    tiles = size.rows // TILE
    pieces = min(len(steps), tiles)
    moments = []
    done = 0
    for piece in range(pieces):
        pivot.start()
        if piece % 2 == 0:
            lu.start()
        count = (tiles - done) // (pieces - piece)
        moments.append(
            call(
                functools.partial(fill_kernel, size, done),
                out_shape=struct(2, 3, count * TILE, SLAB),
                in_specs=[VMEM_WHOLE] * 2,
                out_specs=VMEM_WHOLE,
                cost_estimate=cost(3 * count),
                compiler_params=pltpu.CompilerParams(vmem_limit_bytes=SMALL),
                name=f"fill_slab_{piece}",
            )(test, source)
        )
        done += count
        test = pivot.settle(test)
        if piece % 2 == 1:
            test = lu.settle(test)
    while pivot.left():
        pivot.start()
    while lu.left():
        lu.start()

    tile = call(
        functools.partial(finish_kernel, size, pieces, lu.order, pivot.order),
        out_shape=struct(pcol, size.rows, 2 * size.per_column),
        in_specs=[VMEM_WHOLE] * (pieces + 6),
        out_specs=VMEM_WHOLE,
        scratch_shapes=[
            pltpu.VMEM((2, size.panel, size.panel), F32),
            pltpu.VMEM((2, size.panel, size.panel), F32),
            pltpu.VMEM((size.panel, 2 * size.block), F32),
        ],
        cost_estimate=cost(4),
        compiler_params=pltpu.CompilerParams(vmem_limit_bytes=LARGE),
        name="finish_slab",
    )(*moments, select, length, lu.held, lu.other, pivot.held, pivot.other)
    tile = tile.reshape(pcol * size.rows, 2 * size.per_column)
    return lax.all_to_all(tile, "pcol", 0, 0, tiled=True)


def solution(mesh):
    in_specs = (
        P(None, ("prow", "pcol")),
        P(None, "prow"),
        P(None, "prow"),
        P(),
        P(None, None, "prow", None),
        P(None, None, "prow", None),
    )

    def body(tri_corners, edge_tris, edge_free, pivots, lower_inv, upper_inv):
        size = Sizes(mesh, tri_corners.shape[1], pivots.shape[1])
        return per_device(size, tri_corners, edge_tris, edge_free, pivots, lower_inv, upper_inv)

    return jax.shard_map(
        body, mesh=mesh, in_specs=in_specs, out_specs=P("prow", "pcol"), check_vma=False
    )
```
